32 devices in a mesh: rep: 8 (over y, x, core), shard: 4 (over z).
Axes of the slice: x: 2, y: 2, z: 4, core: 2. Of those that a mesh axis runs over, the one named last changes fastest.
Arguments:
- inputs: bfloat16 [2, 32, 1024, 768], P(None, None, ('rep', 'shard')), may hold values from -6 to 6
- cotangent: bfloat16 [2, 32, 1024, 768], P(None, ('rep', 'shard')), may hold values from -6 to 6
- lengths: int32 [2, 32], replicated, may hold values from 64 to 1024, as said below
- order: int32 [2, 32], replicated, may hold values from 0 to 31, each once within a row
- random_blocks: int32 [2, 32, 12, 16, 3], replicated, may hold values from 0 to 15
- w_qkv: bfloat16 [768, 2304], P('shard'), may hold values from -0.21875 to 0.21875
- bias_query: bfloat16 [768], P('shard'), may hold values from -3 to 3
- bias_value: bfloat16 [768], P('shard'), may hold values from -3 to 3
- w_out: bfloat16 [768, 768], P('shard'), may hold values from -3.5 to 3.5
- bias_out: bfloat16 [768], P('shard'), may hold values from -3 to 3
- gain_first: bfloat16 [768], P('shard'), may hold values from 0.25 to 1.75
- shift_first: bfloat16 [768], P('shard'), may hold values from -3 to 3
- w_up: bfloat16 [768, 3072], P('shard'), may hold values from -0.21875 to 0.21875
- bias_up: bfloat16 [3072], P('shard'), may hold values from -3 to 3
- w_down: bfloat16 [3072, 768], P('shard'), may hold values from -0.109375 to 0.109375
- bias_down: bfloat16 [768], P('shard'), may hold values from -3 to 3
- gain_second: bfloat16 [768], P('shard'), may hold values from 0.25 to 1.75
- shift_second: bfloat16 [768], P('shard'), may hold values from -3 to 3
Outputs:
- output: bfloat16 [2, 32, 1024, 768], P(None, None, ('rep', 'shard'))
- grad_input: bfloat16 [2, 32, 1024, 768], P(None, None, ('rep', 'shard'))
- grad_w_qkv: float32 [768, 2304], P('shard')
- grad_bias_query: float32 [768], P('shard')
- grad_bias_value: float32 [768], P('shard')
- grad_w_out: float32 [768, 768], P('shard')
- grad_bias_out: float32 [768], P('shard')
- grad_gain_first: float32 [768], P('shard')
- grad_shift_first: float32 [768], P('shard')
- grad_w_up: float32 [768, 3072], P('shard')
- grad_bias_up: float32 [3072], P('shard')
- grad_w_down: float32 [3072, 768], P('shard')
- grad_bias_down: float32 [768], P('shard')
- grad_gain_second: float32 [768], P('shard')
- grad_shift_second: float32 [768], P('shard')
The draws below stay inside these ranges and needn't reach their ends.
Inputs may be any that keep to these rules, and one draw needn't show every extreme that they name: `lengths`: in each micro-batch some sequence has 1024 tokens. `order`: each row is a permutation of the sequences of the micro-batch.
All inputs are finite; a program needn't handle non-finite values.
Results may differ from the reference program's by a relative error of at most 0.018.
Values may be sent and summed in bfloat16 or wider, within the bound.
No kernel may reach another device: no remote copies, remote signals or barrier semaphores. Data moves between devices by JAX's collectives and lax.ppermute only.
A program may use at most 320 MiB of HBM per device.

```python
import jax
import jax.numpy as jnp
from jax import lax

D = 768
HEADS = 12
HD = 64
FF = 3072
BLOCK = 64
RANDOM = 3
LEN = 1024
MB = 2
SEQS = 32
NB = 16


def draw_lengths(key, part):
    first_key, second_key = jax.random.split(key)
    drawn_lengths = jax.random.randint(first_key, (MB, SEQS), LEN // 16, LEN + 1, dtype=jnp.int32)
    longest = jax.random.randint(second_key, (MB, 1), 0, SEQS, dtype=jnp.int32)
    positions = jnp.arange(SEQS, dtype=jnp.int32)[None, :]
    return jnp.where(positions == longest, LEN, drawn_lengths).astype(jnp.int32)


def touch_ends(drawn, own_key, least, largest):
    shape = drawn.shape
    place = [jax.random.randint(jax.random.fold_in(own_key, axis), (), 0, shape[axis]) for axis in range(len(shape))]
    drawn = drawn.at[tuple(place)].set(least)
    longest = shape.index(max(shape))
    place[longest] = (place[longest] + 1) % shape[longest]
    return drawn.at[tuple(place)].set(largest)


def levels(key, shape, cuts, smallest, largest):
    gain, own = 1.0, jax.random.fold_in(key, 6)
    for dim, shards_of in cuts:
        draws = jnp.exp(jax.random.uniform(jax.random.fold_in(own, dim), (shards_of,), jnp.float32, smallest / len(cuts), largest / len(cuts)))
        gain = gain * jnp.repeat(draws, shape[dim] // shards_of).reshape([-1 if axis == dim else 1 for axis in range(len(shape))])
    return gain


def normal_values(rng, extent, scale, reach, pieces=(), held_as=jnp.bfloat16):
    values = jax.random.normal(rng, extent, jnp.float32) * scale
    if len(pieces) > 0:
        values = levels(rng, extent, pieces, -0.22, 0.18) * values
    return jnp.clip(values, min=-reach, max=reach).astype(held_as)


def setup_inputs(seed: int = 0) -> dict:
    keys = jax.random.split(jax.random.key(seed), 19)
    return {
        "inputs": normal_values(keys[0], (MB, SEQS, LEN, D), 1.0, 6.0, ((2, 32),)),
        "cotangent": normal_values(keys[1], (MB, SEQS, LEN, D), 1.0, 6.0, ((1, 32),)),
        "lengths": draw_lengths(jax.random.fold_in(keys[18], 71), 0),
        "order": jax.vmap(lambda own: jax.random.permutation(own, SEQS))(jax.random.split(keys[3], MB)).reshape((MB, SEQS)).astype(jnp.int32),
        "random_blocks": touch_ends(jax.random.randint(keys[4], (MB, SEQS, HEADS, NB, RANDOM), 0, LEN // BLOCK), jax.random.fold_in(keys[4], 1), 0, (LEN // BLOCK) - 1).astype(jnp.int32),
        "w_qkv": normal_values(keys[5], (D, 3 * D), D ** -0.5, 0.21875, ((0, 4),)),
        "bias_query": normal_values(keys[6], (D,), 0.5, 3.0, ((0, 4),)),
        "bias_value": normal_values(keys[7], (D,), 0.5, 3.0, ((0, 4),)),
        "w_out": normal_values(keys[8], (D, D), (max(D // 256, 1)) ** -0.5, 3.5, ((0, 4),)),
        "bias_out": normal_values(keys[9], (D,), 0.5, 3.0, ((0, 4),)),
        "gain_first": jnp.clip(1.0 + 0.15 * jax.random.normal(keys[10], (D,), jnp.float32), 0.25, 1.75).astype(jnp.bfloat16),
        "shift_first": normal_values(keys[11], (D,), 0.5, 3.0, ((0, 4),)),
        "w_up": normal_values(keys[12], (D, FF), D ** -0.5, 0.21875, ((0, 4),)),
        "bias_up": normal_values(keys[13], (FF,), 0.5, 3.0, ((0, 4),)),
        "w_down": normal_values(keys[14], (FF, D), FF ** -0.5, 0.109375, ((0, 4),)),
        "bias_down": normal_values(keys[15], (D,), 0.5, 3.0, ((0, 4),)),
        "gain_second": jnp.clip(1.0 + 0.15 * jax.random.normal(keys[16], (D,), jnp.float32), 0.25, 1.75).astype(jnp.bfloat16),
        "shift_second": normal_values(keys[17], (D,), 0.5, 3.0, ((0, 4),)),
    }


@jax.custom_vjp
def low(v):
    return lax.optimization_barrier(v.astype(jnp.bfloat16)).astype(jnp.float32)

@jax.custom_vjp
def low_back(v):
    return v

def low_keep(v):
    return (low(v), None)

def low_pass(kept, grad):
    return (grad,)

def back_keep(v):
    return (v, None)

def back_low(kept, grad):
    return (low(grad),)
low.defvjp(low_keep, low_pass)
low_back.defvjp(back_keep, back_low)
epsilon = 1e-06
masked_score = -1e+30

def layer_norm(hidden, norm_gain, norm_shift):
    center = hidden - lax.optimization_barrier(jnp.mean(hidden, axis=-1, keepdims=True))
    spread = lax.optimization_barrier(jnp.mean(center * center, axis=-1, keepdims=True))
    return center * lax.rsqrt(spread + epsilon) * norm_gain + norm_shift

def block_table(chosen):
    block_count = chosen.shape[1]
    query_block = jnp.arange(block_count, dtype=jnp.int32)[:, None]
    key_block = jnp.arange(block_count, dtype=jnp.int32)[None, :]
    last_block = block_count - 1
    global_rows = (query_block == 0) | (query_block == last_block)
    global_cols = (key_block == 0) | (key_block == last_block)
    fixed_blocks = global_rows | global_cols | (jnp.abs(query_block - key_block) <= 1)
    picked = jnp.any(chosen[:, :, :, None] == key_block[None, None, :, :], axis=2)
    return fixed_blocks[None, :, :] | picked

def block_rows(allowed_table, row_start, row_count, length):
    head_count = allowed_table.shape[0]
    block_count = allowed_table.shape[2]
    table_rows = lax.dynamic_slice_in_dim(allowed_table, row_start // BLOCK, row_count // BLOCK, 1)
    spread_mask = jnp.broadcast_to(table_rows[:, :, None, :, None], (head_count, row_count // BLOCK, BLOCK, block_count, BLOCK))
    spread_mask = spread_mask.reshape(head_count, row_count, block_count * BLOCK)
    live_keys = jnp.arange(block_count * BLOCK, dtype=jnp.int32) < length
    return spread_mask & live_keys[None, None, :]

def attend(projected, allowed_table, length):
    row_count = min(512, LEN)
    scale = HD ** (-0.5)
    key_heads = projected[:, D:2 * D].reshape(LEN, HEADS, HD)
    value_heads = projected[:, 2 * D:].reshape(LEN, HEADS, HD)
    query_part = projected[:, :D]

    def one_block(row_start):
        queries = lax.dynamic_slice_in_dim(query_part, row_start, row_count, 0).reshape(row_count, HEADS, HD)
        allowed = block_rows(allowed_table, row_start, row_count, length)
        raw_scores = jnp.einsum('qhd,khd->hqk', queries, key_heads, precision=lax.Precision.HIGHEST)
        scores = jnp.where(allowed, scale * low_back(raw_scores), masked_score)
        weights = jax.nn.softmax(scores, axis=-1)
        context = jnp.einsum('hqk,khd->qhd', low(weights), value_heads, precision=lax.Precision.HIGHEST)
        live_rows = row_start + jnp.arange(row_count, dtype=jnp.int32) < length
        return context.reshape(row_count, D) * live_rows[:, None].astype(jnp.float32)
    starts = jnp.arange(LEN // row_count, dtype=jnp.int32) * row_count
    return lax.map(jax.checkpoint(one_block), starts).reshape(LEN, D)

def layer(params, tokens, length, chosen):
    w_qkv, bias_query, bias_value, w_out, bias_out, gain_first, shift_first, w_up, bias_up, w_down, bias_down, gain_second, shift_second = params
    highest = lax.Precision.HIGHEST
    bias_all = jnp.concatenate([bias_query, jnp.zeros_like(bias_query), bias_value])
    projected = low(low_back(jnp.dot(tokens, w_qkv, precision=highest)) + bias_all)
    context = low(low_back(attend(projected, block_table(chosen), length)))
    attn_mixed = low_back(jnp.dot(context, w_out, precision=highest)) + bias_out
    normed = layer_norm(tokens + attn_mixed, gain_first, shift_first)
    lifted = low_back(jnp.dot(low(normed), w_up, precision=highest)) + bias_up
    activated = low(jax.nn.gelu(lifted, approximate=False))
    lowered = low_back(jnp.dot(activated, w_down, precision=highest)) + bias_down
    return layer_norm(normed + lowered, gain_second, shift_second)

def reference(inputs, cotangent, lengths, order, random_blocks, w_qkv, bias_query, bias_value, w_out, bias_out, gain_first, shift_first, w_up, bias_up, w_down, bias_down, gain_second, shift_second):
    params = tuple((param.astype(jnp.float32) for param in (w_qkv, bias_query, bias_value, w_out, bias_out, gain_first, shift_first, w_up, bias_up, w_down, bias_down, gain_second, shift_second)))
    inverse = jnp.argsort(order, axis=1).astype(jnp.int32)

    def one_batch(grad_sums, batch_items):
        batch_inputs, batch_cotangent, batch_lengths, batch_order, batch_blocks, batch_inverse = batch_items

        def one_sequence(running, slot):
            source = batch_order[slot]
            tokens = lax.dynamic_index_in_dim(batch_inputs, source, 0, keepdims=False).astype(jnp.float32)
            length = lax.dynamic_index_in_dim(batch_lengths, source, 0, keepdims=False)
            chosen = lax.dynamic_index_in_dim(batch_blocks, source, 0, keepdims=False)
            seq_cotangent = lax.dynamic_index_in_dim(batch_cotangent, slot, 0, keepdims=False).astype(jnp.float32)

            def forward_seq(param_set, token_rows):
                return layer(param_set, token_rows, length, chosen)
            result, pullback = jax.vjp(forward_seq, params, tokens)
            grad_params, grad_tokens = pullback(seq_cotangent)
            running = jax.tree.map(lambda summed, extra: summed + extra, running, grad_params)
            return (running, (result.astype(jnp.bfloat16), grad_tokens.astype(jnp.bfloat16)))
        grad_sums, (results, grad_rows) = lax.scan(one_sequence, grad_sums, jnp.arange(SEQS, dtype=jnp.int32))
        return (grad_sums, (jnp.take(results, batch_inverse, axis=0), jnp.take(grad_rows, batch_inverse, axis=0)))
    zeros = tuple((jnp.zeros(param.shape, jnp.float32) for param in params))
    grad_sums, (outputs, grad_inputs) = lax.scan(one_batch, zeros, (inputs, cotangent, lengths, order, random_blocks, inverse))
    return (outputs, grad_inputs, grad_sums[0], grad_sums[1], grad_sums[2], grad_sums[3], grad_sums[4], grad_sums[5], grad_sums[6], grad_sums[7], grad_sums[8], grad_sums[9], grad_sums[10], grad_sums[11], grad_sums[12])
```

```python
import functools

import jax
import jax.numpy as jnp
from jax import lax
from jax.experimental import pallas as pl
from jax.experimental.pallas import tpu as pltpu
from jax.sharding import PartitionSpec as P

D = 768
HEADS = 12
HD = 64
FF = 3072
BLOCK = 64
LEN = 1024
NB = LEN // BLOCK
PAIRS = HEADS // 2
CHUNK = 256
PARTS = LEN // CHUNK
TILE = 256
EPS = 1e-06
MASKED = -1e30
BOTH = ("rep", "shard")
BF = jnp.bfloat16
F32 = jnp.float32
VMEM_LIMIT = 60 * 1024 * 1024


def nt(a, b):
    return lax.dot_general(a, b, (((1,), (1,)), ((), ())), preferred_element_type=F32)


def nn(a, b):
    return lax.dot_general(a, b, (((1,), (0,)), ((), ())), preferred_element_type=F32)


def tn(a, b):
    return lax.dot_general(a, b, (((0,), (0,)), ((), ())), preferred_element_type=F32)


def mask_rows(chosen):
    i = jnp.arange(NB, dtype=jnp.int32)[:, None]
    j = jnp.arange(NB, dtype=jnp.int32)[None, :]
    fixed = (i == 0) | (i == NB - 1) | (j == 0) | (j == NB - 1) | (jnp.abs(i - j) <= 1)
    picked = jnp.any(chosen[:, :, :, None] == j[None, None], axis=2)
    table = jnp.where(fixed[None] | picked, 0.0, MASKED).astype(F32)
    ends = jnp.full((HEADS, NB, 1), MASKED, F32)
    rest = jnp.zeros((HEADS, NB, 128 - NB - 1), F32)
    return jnp.concatenate([table, ends, rest], axis=2)


def key_columns(length):
    row = lax.broadcasted_iota(jnp.int32, (LEN, 128), 0)
    col = lax.broadcasted_iota(jnp.int32, (LEN, 128), 1)
    hot = ((col < NB) & (row // BLOCK == col)) | ((col == NB) & (row >= length))
    return hot.astype(BF)


def fill_operands(q_ref, k_ref, rows_ref, cols_ref, qa, ka):
    lane = lax.broadcasted_iota(jnp.int32, (1, 128), 1)
    q = q_ref[...].astype(F32) * (HD**-0.5)
    qa[0, :, :128] = jnp.where(lane < HD, q, 0.0).astype(BF)
    qa[1, :, :128] = jnp.where(lane >= HD, q, 0.0).astype(BF)
    for a in range(2):
        for i in range(NB):
            row = jnp.broadcast_to(rows_ref[a, i : i + 1, :], (BLOCK, 128))
            qa[a, i * BLOCK : (i + 1) * BLOCK, 128:] = row.astype(BF)
    ka[:, :128] = k_ref[...]
    ka[:, 128:] = cols_ref[...]


def attend_kernel(len_ref, q_ref, k_ref, v_ref, rows_ref, cols_ref, c_ref, lse_ref, qa, ka, stat):
    step = pl.program_id(0)
    length = len_ref[0]
    fill_operands(q_ref, k_ref, rows_ref, cols_ref, qa, ka)
    lane = lax.broadcasted_iota(jnp.int32, (CHUNK, 128), 1)
    parts = (length + CHUNK - 1) // CHUNK

    @pl.when(step == 0)
    def _():
        stat[...] = jnp.zeros_like(stat)

    def run(count):
        keys = count * CHUNK

        def body(c, carry):
            start = pl.multiple_of(c * CHUNK, CHUNK)
            here = pl.ds(start, CHUNK)
            outs = []
            held = stat[here, :]
            for a in range(2):
                s = nt(qa[a, here, :], ka[:keys, :])
                top = jnp.max(s, axis=1, keepdims=True)
                p = jnp.exp(s - top)
                total = jnp.sum(p, axis=1, keepdims=True)
                outs.append(nn(p.astype(BF), v_ref[:keys, :]) * (1.0 / total))
                held = jnp.where(lane == 2 * step + a, top + jnp.log(total), held)
            stat[here, :] = held
            row = start + lax.broadcasted_iota(jnp.int32, (CHUNK, 128), 0)
            out = jnp.where(lane < HD, outs[0], outs[1])
            c_ref[here, :] = jnp.where(row < length, out, 0.0).astype(BF)
            return carry

        lax.fori_loop(0, count, body, 0)
        if keys < LEN:
            c_ref[keys:, :] = jnp.zeros((LEN - keys, 128), BF)

    for count in range(1, PARTS + 1):
        pl.when(parts == count)(functools.partial(run, count))

    @pl.when(step == PAIRS - 1)
    def _():
        lse_ref[...] = stat[...].T[:16, :]


def attend(projected, rows, cols, length):
    pair = lambda base: pl.BlockSpec((LEN, 128), lambda h, n: (0, base + h))
    return pl.pallas_call(
        attend_kernel,
        name="attend",
        grid_spec=pltpu.PrefetchScalarGridSpec(
            num_scalar_prefetch=1,
            grid=(PAIRS,),
            in_specs=[
                pair(0),
                pair(PAIRS),
                pair(2 * PAIRS),
                pl.BlockSpec((2, NB, 128), lambda h, n: (h, 0, 0)),
                pl.BlockSpec((LEN, 128), lambda h, n: (0, 0)),
            ],
            out_specs=[pair(0), pl.BlockSpec((16, LEN), lambda h, n: (0, 0))],
            scratch_shapes=[
                pltpu.VMEM((2, LEN, 256), BF),
                pltpu.VMEM((LEN, 256), BF),
                pltpu.VMEM((LEN, 128), F32),
            ],
        ),
        out_shape=[jax.ShapeDtypeStruct((LEN, D), BF), jax.ShapeDtypeStruct((16, LEN), F32)],
        compiler_params=pltpu.CompilerParams(vmem_limit_bytes=VMEM_LIMIT),
        cost_estimate=pl.CostEstimate(flops=12 * 10**9, transcendentals=12 * 2**20, bytes_accessed=7 * 2**20),
    )(length, projected, projected, projected, rows, cols)


def attend_back_kernel(
    len_ref, q_ref, k_ref, v_ref, c_ref, g_ref, rows_ref, cols_ref, lse_ref, d_ref, sum_ref, qa, ka, ga, kt, delta, dq, dk, dv
):
    step = pl.program_id(0)
    length = len_ref[0]
    fill_operands(q_ref, k_ref, rows_ref, cols_ref, qa, ka)
    lane = lax.broadcasted_iota(jnp.int32, (1, 128), 1)
    g = g_ref[...].astype(F32)
    ga[0] = jnp.where(lane < HD, g, 0.0).astype(BF)
    ga[1] = jnp.where(lane >= HD, g, 0.0).astype(BF)
    prod = (g * c_ref[...].astype(F32)).T
    delta[0:1, :] = jnp.sum(prod[:HD], axis=0, keepdims=True)
    delta[1:2, :] = jnp.sum(prod[HD:], axis=0, keepdims=True)
    kt[...] = k_ref[...].astype(F32).T.astype(BF)
    dq[...] = jnp.zeros_like(dq)
    dk[...] = jnp.zeros_like(dk)
    dv[...] = jnp.zeros_like(dv)
    parts = (length + CHUNK - 1) // CHUNK

    def run(count):
        keys = count * CHUNK

        def body(c, carry):
            start = pl.multiple_of(c * CHUNK, CHUNK)
            here = pl.ds(start, CHUNK)
            for a in range(2):
                queries = qa[a, here, :]
                grads = ga[a, here, :]
                p = jnp.exp(nt(ka[:keys, :], queries) - lse_ref[pl.ds(2 * step + a, 1), here])
                ds = p * (nt(v_ref[:keys, :], grads) - delta[a : a + 1, here])
                p = p.astype(BF)
                ds = ds.astype(BF)
                dv[:keys, :] += nn(p, grads)
                dk[:keys, :] += nn(ds, queries[:, :128])
                dq[a * HD : (a + 1) * HD, here] = nn(kt[a * HD : (a + 1) * HD, :keys], ds)
            return carry

        lax.fori_loop(0, count, body, 0)

    for count in range(1, PARTS + 1):
        pl.when(parts == count)(functools.partial(run, count))

    grad_q = dq[...].T * (HD**-0.5)
    d_ref[0] = grad_q.astype(BF)
    d_ref[1] = dk[...].astype(BF)
    grad_v = dv[...]
    d_ref[2] = grad_v.astype(BF)
    sum_ref[0:1, :] = jnp.sum(grad_q, axis=0, keepdims=True)
    sum_ref[1:2, :] = jnp.sum(grad_v, axis=0, keepdims=True)
    sum_ref[2:8, :] = jnp.zeros((6, 128), F32)


def attend_back(projected, context, grads, rows, cols, lse, length):
    pair = lambda base: pl.BlockSpec((LEN, 128), lambda h, n: (0, base + h))
    return pl.pallas_call(
        attend_back_kernel,
        name="attend_back",
        grid_spec=pltpu.PrefetchScalarGridSpec(
            num_scalar_prefetch=1,
            grid=(PAIRS,),
            in_specs=[
                pair(0),
                pair(PAIRS),
                pair(2 * PAIRS),
                pair(0),
                pair(0),
                pl.BlockSpec((2, NB, 128), lambda h, n: (h, 0, 0)),
                pl.BlockSpec((LEN, 128), lambda h, n: (0, 0)),
                pl.BlockSpec((16, LEN), lambda h, n: (0, 0)),
            ],
            out_specs=[
                pl.BlockSpec((3, LEN, 128), lambda h, n: (0, 0, h)),
                pl.BlockSpec((8, 128), lambda h, n: (0, h)),
            ],
            scratch_shapes=[
                pltpu.VMEM((2, LEN, 256), BF),
                pltpu.VMEM((LEN, 256), BF),
                pltpu.VMEM((2, LEN, 128), BF),
                pltpu.VMEM((128, LEN), BF),
                pltpu.VMEM((8, LEN), F32),
                pltpu.VMEM((128, LEN), F32),
                pltpu.VMEM((LEN, 128), F32),
                pltpu.VMEM((LEN, 128), F32),
            ],
        ),
        out_shape=[jax.ShapeDtypeStruct((3, LEN, D), BF), jax.ShapeDtypeStruct((8, D), F32)],
        compiler_params=pltpu.CompilerParams(vmem_limit_bytes=VMEM_LIMIT),
        cost_estimate=pl.CostEstimate(flops=30 * 10**9, transcendentals=12 * 2**20, bytes_accessed=15 * 2**20),
    )(length, projected, projected, projected, context, grads, rows, cols, lse)


def gelu_parts(u):
    e = jnp.exp(-0.5 * u * u)
    t = 1.0 / (1.0 + (0.3275911 * 0.7071067811865476) * jnp.abs(u))
    poly = t * (0.127414796 + t * (-0.142248368 + t * (0.7107068705 + t * (-0.7265760135 + t * 0.5307027145))))
    tail = poly * e
    cdf = jnp.where(u >= 0, 1.0 - tail, tail)
    return u * cdf, cdf + u * (0.3989422804014327 * e)


def norm(hidden):
    center = hidden - jnp.mean(hidden, axis=-1, keepdims=True)
    inv = lax.rsqrt(jnp.mean(center * center, axis=-1, keepdims=True) + EPS)
    return center * inv, inv


def norm_back(grad, unit, inv, gain):
    e = gain * grad
    return inv * (e - jnp.mean(e, axis=-1, keepdims=True) - unit * jnp.mean(e * unit, axis=-1, keepdims=True))


def feed_kernel(
    len_ref, c_ref, x_ref, dy_ref, wo_ref, wu_ref, wd_ref, vec_ref, bu_ref,
    y_ref, n_ref, g_ref, dh2_ref, du_ref, dh1_ref, dc_ref, sums_ref, sumu_ref, slope
):
    step = pl.program_id(0)

    @pl.when(step == 0)
    def _():
        sums_ref[...] = jnp.zeros_like(sums_ref)
        sumu_ref[...] = jnp.zeros_like(sumu_ref)

    bias_out, gain1, shift1 = vec_ref[0:1, :], vec_ref[1:2, :], vec_ref[2:3, :]
    bias_down, gain2, shift2 = vec_ref[3:4, :], vec_ref[4:5, :], vec_ref[5:6, :]
    z1, r1 = norm(x_ref[...].astype(F32) + nn(c_ref[...], wo_ref[...]) + bias_out)
    n1 = z1 * gain1 + shift1
    low = n1.astype(BF)
    n_ref[...] = low
    total = n1 + bias_down
    for j in range(FF // D):
        cols = slice(j * D, (j + 1) * D)
        act, der = gelu_parts(nn(low, wu_ref[:, cols]) + bu_ref[:, cols])
        act = act.astype(BF)
        g_ref[:, cols] = act
        slope[:, cols] = der
        total = total + nn(act, wd_ref[cols, :])
    z2, r2 = norm(total)
    y_ref[...] = (z2 * gain2 + shift2).astype(BF)
    dy = dy_ref[...].astype(F32)
    dh2 = norm_back(dy, z2, r2, gain2)
    low = dh2.astype(BF)
    dh2_ref[...] = low
    sums_ref[5:6, :] += jnp.sum(dy * z2, axis=0, keepdims=True)
    sums_ref[6:7, :] += jnp.sum(dy, axis=0, keepdims=True)
    sums_ref[4:5, :] += jnp.sum(dh2, axis=0, keepdims=True)
    total = dh2
    for j in range(FF // D):
        cols = slice(j * D, (j + 1) * D)
        du = nt(low, wd_ref[cols, :]) * slope[:, cols]
        sumu_ref[0:1, cols] += jnp.sum(du, axis=0, keepdims=True)
        du = du.astype(BF)
        du_ref[:, cols] = du
        total = total + nt(du, wu_ref[:, cols])
    dh1 = norm_back(total, z1, r1, gain1)
    sums_ref[2:3, :] += jnp.sum(total * z1, axis=0, keepdims=True)
    sums_ref[3:4, :] += jnp.sum(total, axis=0, keepdims=True)
    sums_ref[1:2, :] += jnp.sum(dh1, axis=0, keepdims=True)
    low = dh1.astype(BF)
    dh1_ref[...] = low
    row = step * TILE + lax.broadcasted_iota(jnp.int32, (TILE, 1), 0)
    dc_ref[...] = jnp.where(row < len_ref[0], nt(low, wo_ref[...]), 0.0).astype(BF)


def feed(context, tokens, cotangent, w_out, w_up, w_down, vectors, bias_up, length):
    whole = lambda *shape: pl.BlockSpec(shape, lambda i, n: (0, 0), pipeline_mode=pl.Buffered(1))
    fixed = lambda *shape: pl.BlockSpec(shape, lambda i, n: (0, 0))
    tile = lambda width: pl.BlockSpec((TILE, width), lambda i, n: (i, 0))
    narrow = jax.ShapeDtypeStruct((LEN, D), BF)
    wide = jax.ShapeDtypeStruct((LEN, FF), BF)
    return pl.pallas_call(
        feed_kernel,
        name="feed",
        grid_spec=pltpu.PrefetchScalarGridSpec(
            num_scalar_prefetch=1,
            grid=(LEN // TILE,),
            in_specs=[
                tile(D), tile(D), tile(D), whole(D, D), whole(D, FF), whole(FF, D), fixed(8, D), fixed(1, FF)
            ],
            out_specs=[
                tile(D), tile(D), tile(FF), tile(D), tile(FF), tile(D), tile(D), fixed(8, D), fixed(8, FF)
            ],
            scratch_shapes=[pltpu.VMEM((TILE, FF), F32)],
        ),
        out_shape=[
            narrow, narrow, wide, narrow, wide, narrow, narrow,
            jax.ShapeDtypeStruct((8, D), F32), jax.ShapeDtypeStruct((8, FF), F32)
        ],
        compiler_params=pltpu.CompilerParams(vmem_limit_bytes=VMEM_LIMIT),
        cost_estimate=pl.CostEstimate(flops=22 * 10**9, transcendentals=3 * 2**20, bytes_accessed=36 * 2**20),
    )(length, context, tokens, cotangent, w_out, w_up, w_down, vectors, bias_up)


def tokens_back_kernel(d_ref, h_ref, w_ref, x_ref):
    total = h_ref[...].astype(F32)
    for j in range(3):
        total = total + nt(d_ref[j], w_ref[:, j * D : (j + 1) * D])
    x_ref[...] = total.astype(BF)


def tokens_back(grads, hidden, w_qkv):
    return pl.pallas_call(
        tokens_back_kernel,
        name="tokens_back",
        grid=(LEN // TILE,),
        in_specs=[
            pl.BlockSpec((3, TILE, D), lambda i: (0, i, 0)),
            pl.BlockSpec((TILE, D), lambda i: (i, 0)),
            pl.BlockSpec((D, 3 * D), lambda i: (0, 0), pipeline_mode=pl.Buffered(1)),
        ],
        out_specs=pl.BlockSpec((TILE, D), lambda i: (i, 0)),
        out_shape=jax.ShapeDtypeStruct((LEN, D), BF),
        compiler_params=pltpu.CompilerParams(vmem_limit_bytes=VMEM_LIMIT),
        cost_estimate=pl.CostEstimate(flops=4 * 10**9, transcendentals=0, bytes_accessed=12 * 2**20),
    )(grads, hidden, w_qkv)


def gather_rows(weight, rep, reps, shards):
    rows = weight.shape[0] // reps
    mine = lax.dynamic_slice_in_dim(weight, rep * rows, rows, 0)
    whole = lax.all_gather(mine, BOTH, axis=0, tiled=True)
    whole = whole.reshape(reps, shards, rows, weight.shape[1])
    return whole.transpose(1, 0, 2, 3).reshape(shards * reps * rows, weight.shape[1])


def reduce_rows(grad, reps, shards):
    rows = grad.shape[0] // (reps * shards)
    parts = grad.reshape(shards, reps, rows, grad.shape[1]).transpose(1, 0, 2, 3)
    parts = parts.reshape(grad.shape)
    mine = lax.psum_scatter(parts, BOTH, scatter_dimension=0, tiled=True)
    return lax.all_gather(mine, "rep", axis=0, tiled=True).astype(F32)


def per_device(
    inputs, cotangent, lengths, order, random_blocks,
    w_qkv, bias_query, bias_value, w_out, bias_out, gain_first, shift_first,
    w_up, bias_up, w_down, bias_down, gain_second, shift_second,
):
    device = lax.axis_index(BOTH)
    rep = lax.axis_index("rep")
    reps, shards = lax.axis_size("rep"), lax.axis_size("shard")
    seqs = reps * shards
    batches = inputs.shape[0]

    arrived = []
    for m in range(batches):
        sent = jnp.take(inputs[m], order[m], axis=0)
        got = lax.all_to_all(sent, BOTH, split_axis=0, concat_axis=0, tiled=True)
        arrived.append(got.reshape(LEN, D))
    packed = jnp.stack(
        [bias_query, bias_value, bias_out, gain_first, shift_first, bias_down, gain_second, shift_second]
        + list(bias_up.reshape(4, -1)), axis=0
    )
    vectors = lax.all_gather(packed[None], "shard", axis=0, tiled=True).astype(F32)
    small = vectors[:, :8].transpose(1, 0, 2).reshape(8, D)
    lift_bias = vectors[:, 8:].reshape(1, FF)
    feed_vectors = jnp.concatenate([small[2:], jnp.zeros((2, D), F32)], axis=0)
    bias_all = jnp.concatenate([small[0], jnp.zeros((D,), F32), small[1]])
    qkv = gather_rows(w_qkv, rep, reps, shards)
    out = gather_rows(w_out, rep, reps, shards)
    up = gather_rows(w_up, rep, reps, shards)
    down = gather_rows(w_down, rep, reps, shards)

    outputs, saved = [], []
    for m in range(batches):
        source = order[m, device]
        length = lengths[m, source]
        one = length.reshape(1)
        rows = mask_rows(random_blocks[m, source])
        cols = key_columns(length)
        tokens = arrived[m]
        projected = (jnp.dot(tokens, qkv, preferred_element_type=F32) + bias_all).astype(BF)
        context, lse = attend(projected, rows, cols, one)
        y, n1, g, dh2, du, dh1, dc, sums, sumu = feed(
            context, tokens, cotangent[m, 0], out, up, down, feed_vectors, lift_bias, one
        )
        back = lax.all_to_all(y.reshape(seqs, LEN // seqs, D), BOTH, split_axis=0, concat_axis=0, tiled=True)
        outputs.append(jnp.take(back, jnp.argsort(order[m]), axis=0))
        saved.append((projected, context, dc, rows, cols, lse, one, tokens, n1, g, dh2, du, dh1, sums, sumu))

    def both(left, right):
        return sum(tn(s[left], s[right]) for s in saved).astype(BF)

    grad_down = reduce_rows(both(9, 10), reps, shards)
    grad_up = reduce_rows(both(8, 11), reps, shards)
    grad_out = reduce_rows(both(1, 12), reps, shards)

    grad_inputs, grads, bias_sums = [], [], []
    for m in range(batches):
        projected, context, dc, rows, cols, lse, one = saved[m][:7]
        d3, dsum = attend_back(projected, context, dc, rows, cols, lse, one)
        dx = tokens_back(d3, saved[m][12], qkv)
        back = lax.all_to_all(dx.reshape(seqs, LEN // seqs, D), BOTH, split_axis=0, concat_axis=0, tiled=True)
        grad_inputs.append(jnp.take(back, jnp.argsort(order[m]), axis=0))
        grads.append(d3)
        bias_sums.append(dsum)
    grad_qkv = jnp.concatenate(
        [sum(tn(saved[m][7], grads[m][j]) for m in range(batches)).astype(BF) for j in range(3)], axis=1
    )
    grad_qkv = reduce_rows(grad_qkv, reps, shards)

    sums = sum(s[13] for s in saved)
    sumu = sum(s[14] for s in saved)[0].reshape(4, D)
    dsum = sum(bias_sums)
    rows12 = jnp.concatenate([dsum[0:2], sums[1:7], sumu], axis=0)
    rows12 = lax.psum(rows12, BOTH)
    shard = lax.axis_index("shard")
    width = D // shards
    own = lax.dynamic_slice_in_dim(rows12[:8], shard * width, width, 1)
    lift = lax.dynamic_slice_in_dim(rows12[8:].reshape(FF), shard * (FF // shards), FF // shards, 0)
    return (
        jnp.stack(outputs), jnp.stack(grad_inputs),
        grad_qkv, own[0], own[1], grad_out, own[2], own[3], own[4], grad_up, lift, grad_down, own[5], own[6], own[7],
    )


def solution(mesh):
    tokens = P(None, None, BOTH, None)
    placed = (
        tokens, P(None, BOTH, None, None), P(), P(), P(),
        P("shard", None), P("shard"), P("shard"), P("shard", None), P("shard"), P("shard"), P("shard"),
        P("shard", None), P("shard"), P("shard", None), P("shard"), P("shard"), P("shard"),
    )
    return jax.shard_map(
        per_device, mesh=mesh, in_specs=placed, out_specs=(tokens, tokens) + placed[5:], check_vma=False
    )
```

```python
import functools

import jax
import jax.numpy as jnp
from jax import lax
from jax.experimental import pallas as pl
from jax.experimental.pallas import tpu as pltpu
from jax.sharding import PartitionSpec as P

D = 768
HEADS = 12
HD = 64
FF = 3072
BLOCK = 64
LEN = 1024
NB = LEN // BLOCK
PAIRS = HEADS // 2
CHUNK = 256
PARTS = LEN // CHUNK
TILE = 256
EPS = 1e-06
MASKED = -1e30
BOTH = ("rep", "shard")
BF = jnp.bfloat16
F32 = jnp.float32
VMEM_LIMIT = 60 * 1024 * 1024


def nt(a, b):
    return lax.dot_general(a, b, (((1,), (1,)), ((), ())), preferred_element_type=F32)


def nn(a, b):
    return lax.dot_general(a, b, (((1,), (0,)), ((), ())), preferred_element_type=F32)


def tn(a, b):
    return lax.dot_general(a, b, (((0,), (0,)), ((), ())), preferred_element_type=F32)


def mask_rows(chosen):
    i = jnp.arange(NB, dtype=jnp.int32)[:, None]
    j = jnp.arange(NB, dtype=jnp.int32)[None, :]
    fixed = (i == 0) | (i == NB - 1) | (j == 0) | (j == NB - 1) | (jnp.abs(i - j) <= 1)
    picked = jnp.any(chosen[:, :, :, None] == j[None, None], axis=2)
    table = jnp.where(fixed[None] | picked, 0.0, MASKED).astype(F32)
    ends = jnp.full((HEADS, NB, 1), MASKED, F32)
    rest = jnp.zeros((HEADS, NB, 128 - NB - 1), F32)
    return jnp.concatenate([table, ends, rest], axis=2)


def key_columns(length):
    row = lax.broadcasted_iota(jnp.int32, (LEN, 128), 0)
    col = lax.broadcasted_iota(jnp.int32, (LEN, 128), 1)
    hot = ((col < NB) & (row // BLOCK == col)) | ((col == NB) & (row >= length))
    return hot.astype(BF)


def fill_operands(q_ref, k_ref, rows_ref, cols_ref, qa, ka):
    lane = lax.broadcasted_iota(jnp.int32, (1, 128), 1)
    q = q_ref[...].astype(F32) * (HD**-0.5)
    qa[0, :, :128] = jnp.where(lane < HD, q, 0.0).astype(BF)
    qa[1, :, :128] = jnp.where(lane >= HD, q, 0.0).astype(BF)
    for a in range(2):
        for i in range(NB):
            row = jnp.broadcast_to(rows_ref[a, i : i + 1, :], (BLOCK, 128))
            qa[a, i * BLOCK : (i + 1) * BLOCK, 128:] = row.astype(BF)
    ka[:, :128] = k_ref[...]
    ka[:, 128:] = cols_ref[...]


def attend_kernel(len_ref, q_ref, k_ref, v_ref, rows_ref, cols_ref, c_ref, lse_ref, qa, ka, stat):
    step = pl.program_id(0)
    length = len_ref[0]
    fill_operands(q_ref, k_ref, rows_ref, cols_ref, qa, ka)
    lane = lax.broadcasted_iota(jnp.int32, (CHUNK, 128), 1)
    parts = (length + CHUNK - 1) // CHUNK

    @pl.when(step == 0)
    def _():
        stat[...] = jnp.zeros_like(stat)

    def run(count):
        keys = count * CHUNK

        def body(c, carry):
            start = pl.multiple_of(c * CHUNK, CHUNK)
            here = pl.ds(start, CHUNK)
            outs = []
            held = stat[here, :]
            for a in range(2):
                s = nt(qa[a, here, :], ka[:keys, :])
                top = jnp.max(s, axis=1, keepdims=True)
                p = jnp.exp(s - top)
                total = jnp.sum(p, axis=1, keepdims=True)
                outs.append(nn(p.astype(BF), v_ref[:keys, :]) * (1.0 / total))
                held = jnp.where(lane == 2 * step + a, top + jnp.log(total), held)
            stat[here, :] = held
            row = start + lax.broadcasted_iota(jnp.int32, (CHUNK, 128), 0)
            out = jnp.where(lane < HD, outs[0], outs[1])
            c_ref[here, :] = jnp.where(row < length, out, 0.0).astype(BF)
            return carry

        lax.fori_loop(0, count, body, 0)
        if keys < LEN:
            c_ref[keys:, :] = jnp.zeros((LEN - keys, 128), BF)

    for count in range(1, PARTS + 1):
        pl.when(parts == count)(functools.partial(run, count))

    @pl.when(step == PAIRS - 1)
    def _():
        lse_ref[...] = stat[...].T[:16, :]


def attend(projected, rows, cols, length):
    pair = lambda base: pl.BlockSpec((LEN, 128), lambda h, n: (0, base + h))
    return pl.pallas_call(
        attend_kernel,
        name="attend",
        grid_spec=pltpu.PrefetchScalarGridSpec(
            num_scalar_prefetch=1,
            grid=(PAIRS,),
            in_specs=[
                pair(0),
                pair(PAIRS),
                pair(2 * PAIRS),
                pl.BlockSpec((2, NB, 128), lambda h, n: (h, 0, 0)),
                pl.BlockSpec((LEN, 128), lambda h, n: (0, 0)),
            ],
            out_specs=[pair(0), pl.BlockSpec((16, LEN), lambda h, n: (0, 0))],
            scratch_shapes=[
                pltpu.VMEM((2, LEN, 256), BF),
                pltpu.VMEM((LEN, 256), BF),
                pltpu.VMEM((LEN, 128), F32),
            ],
        ),
        out_shape=[jax.ShapeDtypeStruct((LEN, D), BF), jax.ShapeDtypeStruct((16, LEN), F32)],
        compiler_params=pltpu.CompilerParams(vmem_limit_bytes=VMEM_LIMIT),
        cost_estimate=pl.CostEstimate(flops=12 * 10**9, transcendentals=12 * 2**20, bytes_accessed=7 * 2**20),
    )(length, projected, projected, projected, rows, cols)


def attend_back_kernel(
    len_ref, q_ref, k_ref, v_ref, c_ref, g_ref, rows_ref, cols_ref, lse_ref, d_ref, sum_ref, qa, ka, ga, kt, delta, dq, dk, dv
):
    step = pl.program_id(0)
    length = len_ref[0]
    fill_operands(q_ref, k_ref, rows_ref, cols_ref, qa, ka)
    lane = lax.broadcasted_iota(jnp.int32, (1, 128), 1)
    g = g_ref[...].astype(F32)
    ga[0] = jnp.where(lane < HD, g, 0.0).astype(BF)
    ga[1] = jnp.where(lane >= HD, g, 0.0).astype(BF)
    prod = (g * c_ref[...].astype(F32)).T
    delta[0:1, :] = jnp.sum(prod[:HD], axis=0, keepdims=True)
    delta[1:2, :] = jnp.sum(prod[HD:], axis=0, keepdims=True)
    kt[...] = k_ref[...].astype(F32).T.astype(BF)
    dq[...] = jnp.zeros_like(dq)
    dk[...] = jnp.zeros_like(dk)
    dv[...] = jnp.zeros_like(dv)
    parts = (length + CHUNK - 1) // CHUNK

    def run(count):
        keys = count * CHUNK

        def body(c, carry):
            start = pl.multiple_of(c * CHUNK, CHUNK)
            here = pl.ds(start, CHUNK)
            for a in range(2):
                queries = qa[a, here, :]
                grads = ga[a, here, :]
                p = jnp.exp(nt(ka[:keys, :], queries) - lse_ref[pl.ds(2 * step + a, 1), here])
                ds = p * (nt(v_ref[:keys, :], grads) - delta[a : a + 1, here])
                p = p.astype(BF)
                ds = ds.astype(BF)
                dv[:keys, :] += nn(p, grads)
                dk[:keys, :] += nn(ds, queries[:, :128])
                dq[a * HD : (a + 1) * HD, here] = nn(kt[a * HD : (a + 1) * HD, :keys], ds)
            return carry

        lax.fori_loop(0, count, body, 0)

    for count in range(1, PARTS + 1):
        pl.when(parts == count)(functools.partial(run, count))

    grad_q = dq[...].T * (HD**-0.5)
    d_ref[0] = grad_q.astype(BF)
    d_ref[1] = dk[...].astype(BF)
    grad_v = dv[...]
    d_ref[2] = grad_v.astype(BF)
    sum_ref[0:1, :] = jnp.sum(grad_q, axis=0, keepdims=True)
    sum_ref[1:2, :] = jnp.sum(grad_v, axis=0, keepdims=True)
    sum_ref[2:8, :] = jnp.zeros((6, 128), F32)


def attend_back(projected, context, grads, rows, cols, lse, length):
    pair = lambda base: pl.BlockSpec((LEN, 128), lambda h, n: (0, base + h))
    return pl.pallas_call(
        attend_back_kernel,
        name="attend_back",
        grid_spec=pltpu.PrefetchScalarGridSpec(
            num_scalar_prefetch=1,
            grid=(PAIRS,),
            in_specs=[
                pair(0),
                pair(PAIRS),
                pair(2 * PAIRS),
                pair(0),
                pair(0),
                pl.BlockSpec((2, NB, 128), lambda h, n: (h, 0, 0)),
                pl.BlockSpec((LEN, 128), lambda h, n: (0, 0)),
                pl.BlockSpec((16, LEN), lambda h, n: (0, 0)),
            ],
            out_specs=[
                pl.BlockSpec((3, LEN, 128), lambda h, n: (0, 0, h)),
                pl.BlockSpec((8, 128), lambda h, n: (0, h)),
            ],
            scratch_shapes=[
                pltpu.VMEM((2, LEN, 256), BF),
                pltpu.VMEM((LEN, 256), BF),
                pltpu.VMEM((2, LEN, 128), BF),
                pltpu.VMEM((128, LEN), BF),
                pltpu.VMEM((8, LEN), F32),
                pltpu.VMEM((128, LEN), F32),
                pltpu.VMEM((LEN, 128), F32),
                pltpu.VMEM((LEN, 128), F32),
            ],
        ),
        out_shape=[jax.ShapeDtypeStruct((3, LEN, D), BF), jax.ShapeDtypeStruct((8, D), F32)],
        compiler_params=pltpu.CompilerParams(vmem_limit_bytes=VMEM_LIMIT),
        cost_estimate=pl.CostEstimate(flops=30 * 10**9, transcendentals=12 * 2**20, bytes_accessed=15 * 2**20),
    )(length, projected, projected, projected, context, grads, rows, cols, lse)


def gelu_parts(u):
    e = jnp.exp(-0.5 * u * u)
    t = 1.0 / (1.0 + (0.3275911 * 0.7071067811865476) * jnp.abs(u))
    poly = t * (0.127414796 + t * (-0.142248368 + t * (0.7107068705 + t * (-0.7265760135 + t * 0.5307027145))))
    tail = poly * e
    cdf = jnp.where(u >= 0, 1.0 - tail, tail)
    return u * cdf, cdf + u * (0.3989422804014327 * e)


def norm(hidden):
    center = hidden - jnp.mean(hidden, axis=-1, keepdims=True)
    inv = lax.rsqrt(jnp.mean(center * center, axis=-1, keepdims=True) + EPS)
    return center * inv, inv


def norm_back(grad, unit, inv, gain):
    e = gain * grad
    return inv * (e - jnp.mean(e, axis=-1, keepdims=True) - unit * jnp.mean(e * unit, axis=-1, keepdims=True))


def feed_kernel(
    len_ref, c_ref, x_ref, dy_ref, wo_ref, wu_ref, wd_ref, vec_ref, bu_ref,
    y_ref, n_ref, g_ref, dh2_ref, du_ref, dh1_ref, dc_ref, sums_ref, sumu_ref, slope
):
    step = pl.program_id(0)

    @pl.when(step == 0)
    def _():
        sums_ref[...] = jnp.zeros_like(sums_ref)
        sumu_ref[...] = jnp.zeros_like(sumu_ref)

    bias_out, gain1, shift1 = vec_ref[0:1, :], vec_ref[1:2, :], vec_ref[2:3, :]
    bias_down, gain2, shift2 = vec_ref[3:4, :], vec_ref[4:5, :], vec_ref[5:6, :]
    z1, r1 = norm(x_ref[...].astype(F32) + nn(c_ref[...], wo_ref[...]) + bias_out)
    n1 = z1 * gain1 + shift1
    low = n1.astype(BF)
    n_ref[...] = low
    total = n1 + bias_down
    for j in range(FF // D):
        cols = slice(j * D, (j + 1) * D)
        act, der = gelu_parts(nn(low, wu_ref[:, cols]) + bu_ref[:, cols])
        act = act.astype(BF)
        g_ref[:, cols] = act
        slope[:, cols] = der
        total = total + nn(act, wd_ref[cols, :])
    z2, r2 = norm(total)
    y_ref[...] = (z2 * gain2 + shift2).astype(BF)
    dy = dy_ref[...].astype(F32)
    dh2 = norm_back(dy, z2, r2, gain2)
    low = dh2.astype(BF)
    dh2_ref[...] = low
    sums_ref[5:6, :] += jnp.sum(dy * z2, axis=0, keepdims=True)
    sums_ref[6:7, :] += jnp.sum(dy, axis=0, keepdims=True)
    sums_ref[4:5, :] += jnp.sum(dh2, axis=0, keepdims=True)
    total = dh2
    for j in range(FF // D):
        cols = slice(j * D, (j + 1) * D)
        du = nt(low, wd_ref[cols, :]) * slope[:, cols]
        sumu_ref[0:1, cols] += jnp.sum(du, axis=0, keepdims=True)
        du = du.astype(BF)
        du_ref[:, cols] = du
        total = total + nt(du, wu_ref[:, cols])
    dh1 = norm_back(total, z1, r1, gain1)
    sums_ref[2:3, :] += jnp.sum(total * z1, axis=0, keepdims=True)
    sums_ref[3:4, :] += jnp.sum(total, axis=0, keepdims=True)
    sums_ref[1:2, :] += jnp.sum(dh1, axis=0, keepdims=True)
    low = dh1.astype(BF)
    dh1_ref[...] = low
    row = step * TILE + lax.broadcasted_iota(jnp.int32, (TILE, 1), 0)
    dc_ref[...] = jnp.where(row < len_ref[0], nt(low, wo_ref[...]), 0.0).astype(BF)


def feed(context, tokens, cotangent, w_out, w_up, w_down, vectors, bias_up, length):
    whole = lambda *shape: pl.BlockSpec(shape, lambda i, n: (0, 0), pipeline_mode=pl.Buffered(1))
    fixed = lambda *shape: pl.BlockSpec(shape, lambda i, n: (0, 0))
    tile = lambda width: pl.BlockSpec((TILE, width), lambda i, n: (i, 0))
    narrow = jax.ShapeDtypeStruct((LEN, D), BF)
    wide = jax.ShapeDtypeStruct((LEN, FF), BF)
    return pl.pallas_call(
        feed_kernel,
        name="feed",
        grid_spec=pltpu.PrefetchScalarGridSpec(
            num_scalar_prefetch=1,
            grid=(LEN // TILE,),
            in_specs=[
                tile(D), tile(D), tile(D), whole(D, D), whole(D, FF), whole(FF, D), fixed(8, D), fixed(1, FF)
            ],
            out_specs=[
                tile(D), tile(D), tile(FF), tile(D), tile(FF), tile(D), tile(D), fixed(8, D), fixed(8, FF)
            ],
            scratch_shapes=[pltpu.VMEM((TILE, FF), F32)],
        ),
        out_shape=[
            narrow, narrow, wide, narrow, wide, narrow, narrow,
            jax.ShapeDtypeStruct((8, D), F32), jax.ShapeDtypeStruct((8, FF), F32)
        ],
        compiler_params=pltpu.CompilerParams(vmem_limit_bytes=VMEM_LIMIT),
        cost_estimate=pl.CostEstimate(flops=22 * 10**9, transcendentals=3 * 2**20, bytes_accessed=36 * 2**20),
    )(length, context, tokens, cotangent, w_out, w_up, w_down, vectors, bias_up)


def tokens_back_kernel(d_ref, h_ref, w_ref, x_ref):
    total = h_ref[...].astype(F32)
    for j in range(3):
        total = total + nt(d_ref[j], w_ref[:, j * D : (j + 1) * D])
    x_ref[...] = total.astype(BF)


def tokens_back(grads, hidden, w_qkv):
    return pl.pallas_call(
        tokens_back_kernel,
        name="tokens_back",
        grid=(LEN // TILE,),
        in_specs=[
            pl.BlockSpec((3, TILE, D), lambda i: (0, i, 0)),
            pl.BlockSpec((TILE, D), lambda i: (i, 0)),
            pl.BlockSpec((D, 3 * D), lambda i: (0, 0), pipeline_mode=pl.Buffered(1)),
        ],
        out_specs=pl.BlockSpec((TILE, D), lambda i: (i, 0)),
        out_shape=jax.ShapeDtypeStruct((LEN, D), BF),
        compiler_params=pltpu.CompilerParams(vmem_limit_bytes=VMEM_LIMIT),
        cost_estimate=pl.CostEstimate(flops=4 * 10**9, transcendentals=0, bytes_accessed=12 * 2**20),
    )(grads, hidden, w_qkv)


def up8(rows):
    return -(-rows // 8) * 8


def wide_rows(block):
    return jnp.concatenate([block[..., j * D : (j + 1) * D] for j in range(block.shape[-1] // D)], axis=-2)


def rows_wide(block, count):
    reps, shards, rows = block.shape[0], block.shape[1], block.shape[2] // count
    block = block.reshape(reps, shards, count, rows, D).transpose(1, 0, 3, 2, 4)
    return block.reshape(shards * reps * rows, count * D)


def parts_of(grad, reps, shards):
    return grad.reshape(shards, reps, -1, D).transpose(1, 0, 2, 3)


def per_device(
    inputs, cotangent, lengths, order, random_blocks,
    w_qkv, bias_query, bias_value, w_out, bias_out, gain_first, shift_first,
    w_up, bias_up, w_down, bias_down, gain_second, shift_second,
):
    device = lax.axis_index(BOTH)
    rep = lax.axis_index("rep")
    reps, shards = lax.axis_size("rep"), lax.axis_size("shard")
    seqs = reps * shards
    batches = inputs.shape[0]

    arrived = []
    for m in range(batches):
        sent = jnp.take(inputs[m], order[m], axis=0)
        got = lax.all_to_all(sent, BOTH, split_axis=0, concat_axis=0, tiled=True)
        arrived.append(got.reshape(LEN, D))
    part = lambda weight: lax.dynamic_slice_in_dim(weight, rep * (weight.shape[0] // reps), weight.shape[0] // reps, 0)
    rows = D // seqs
    packed = jnp.stack(
        [bias_query, bias_value, bias_out, gain_first, shift_first, bias_down, gain_second, shift_second]
        + list(bias_up.reshape(FF // D, -1)), axis=0
    ).reshape(-1, D)
    extra = packed.shape[0]
    pad = jnp.zeros((up8(3 * rows + extra) - 3 * rows - extra, D), BF)
    first = jnp.concatenate([wide_rows(part(w_qkv)), packed, pad], axis=0)
    first = lax.all_gather(first, BOTH, axis=0).reshape(reps, shards, -1, D)
    qkv = rows_wide(first[:, :, : 3 * rows], 3)
    vectors = first[0, :, 3 * rows : 3 * rows + extra].astype(F32).reshape(shards, -1, D // shards)
    small = vectors[:, :8].transpose(1, 0, 2).reshape(8, D)
    lift_bias = vectors[:, 8:].reshape(1, FF)
    feed_vectors = jnp.concatenate([small[2:], jnp.zeros((2, D), F32)], axis=0)
    bias_all = jnp.concatenate([small[0], jnp.zeros((D,), F32), small[1]])
    rest = jnp.concatenate([part(w_out), wide_rows(part(w_up)), part(w_down)], axis=0)
    rest = lax.all_gather(rest, BOTH, axis=0).reshape(reps, shards, -1, D)
    out = rows_wide(rest[:, :, :rows], 1)
    up = rows_wide(rest[:, :, rows : 5 * rows], 4)
    down = rows_wide(rest[:, :, 5 * rows :], 1)

    outputs, saved = [], []
    for m in range(batches):
        source = order[m, device]
        length = lengths[m, source]
        one = length.reshape(1)
        table = mask_rows(random_blocks[m, source])
        cols = key_columns(length)
        tokens = arrived[m]
        projected = (jnp.dot(tokens, qkv, preferred_element_type=F32) + bias_all).astype(BF)
        context, lse = attend(projected, table, cols, one)
        y, n1, g, dh2, du, dh1, dc, sums, sumu = feed(
            context, tokens, cotangent[m, 0], out, up, down, feed_vectors, lift_bias, one
        )
        back = lax.all_to_all(y.reshape(seqs, LEN // seqs, D), BOTH, split_axis=0, concat_axis=0, tiled=True)
        outputs.append(jnp.take(back, jnp.argsort(order[m]), axis=0))
        saved.append((projected, context, dc, table, cols, lse, one, tokens, n1, g, dh2, du, dh1, sums, sumu))

    def both(left, right):
        return sum(tn(s[left], s[right]) for s in saved).astype(BF)

    grad_up = both(8, 11).reshape(shards, reps, rows, FF).transpose(1, 0, 2, 3)
    parts = jnp.concatenate(
        [parts_of(both(1, 12), reps, shards), wide_rows(grad_up), parts_of(both(9, 10), reps, shards)], axis=2
    )
    mine = lax.psum_scatter(parts.reshape(-1, D), BOTH, scatter_dimension=0, tiled=True)
    mine = lax.all_gather(mine, "rep", axis=0)
    grad_out = rows_wide(mine[:, None, :rows], 1).astype(F32)
    grad_up = rows_wide(mine[:, None, rows : 5 * rows], 4).astype(F32)
    grad_down = rows_wide(mine[:, None, 5 * rows :], 1).astype(F32)

    grad_inputs, grads, bias_sums = [], [], []
    for m in range(batches):
        projected, context, dc, table, cols, lse, one = saved[m][:7]
        d3, dsum = attend_back(projected, context, dc, table, cols, lse, one)
        dx = tokens_back(d3, saved[m][12], qkv)
        back = lax.all_to_all(dx.reshape(seqs, LEN // seqs, D), BOTH, split_axis=0, concat_axis=0, tiled=True)
        grad_inputs.append(jnp.take(back, jnp.argsort(order[m]), axis=0))
        grads.append(d3)
        bias_sums.append(dsum)
    sums = sum(s[13] for s in saved)
    sumu = sum(s[14] for s in saved)[0].reshape(FF // D, D)
    dsum = sum(bias_sums)
    sums = jnp.concatenate([dsum[0:2], sums[1:7]], axis=0).reshape(8, shards, -1).transpose(1, 0, 2)
    sums = jnp.concatenate([sums, sumu.reshape(shards, FF // D, -1)], axis=1).astype(BF).reshape(1, shards, extra, D)
    sums = jnp.broadcast_to(sums, (reps, shards, extra, D))
    blank = jnp.zeros((reps, shards) + pad.shape, BF)
    parts = [
        parts_of(sum(tn(saved[m][7], grads[m][j]) for m in range(batches)).astype(BF), reps, shards) for j in range(3)
    ]
    parts = jnp.concatenate(parts + [sums, blank], axis=2).reshape(seqs, -1, D)
    parts = lax.all_to_all(parts, BOTH, split_axis=0, concat_axis=0, tiled=True)
    mine = jnp.sum(parts.astype(F32), axis=0).astype(BF)
    mine = lax.all_gather(mine, "rep", axis=0)
    grad_qkv = rows_wide(mine[:, None, : 3 * rows], 3).astype(F32)
    own = mine[0, 3 * rows : 3 * rows + extra].astype(F32).reshape(-1, D // shards)
    lift = own[8:].reshape(FF // shards)
    return (
        jnp.stack(outputs), jnp.stack(grad_inputs),
        grad_qkv, own[0], own[1], grad_out, own[2], own[3], own[4], grad_up, lift, grad_down, own[5], own[6], own[7],
    )


def solution(mesh):
    tokens = P(None, None, BOTH, None)
    placed = (
        tokens, P(None, BOTH, None, None), P(), P(), P(),
        P("shard", None), P("shard"), P("shard"), P("shard", None), P("shard"), P("shard"), P("shard"),
        P("shard", None), P("shard"), P("shard", None), P("shard"), P("shard"), P("shard"),
    )
    return jax.shard_map(
        per_device, mesh=mesh, in_specs=placed, out_specs=(tokens, tokens) + placed[5:], check_vma=False
    )
```
